256 devices in a mesh: grp: 2 (over z_hi), mem: 128 (over x, z_lo, y, core).
Axes of the slice: x: 4, y: 4, z: 8 (z_hi: 2, z_lo: 4; z = z_hi * 4 + z_lo), core: 2. Of those that a mesh axis runs over, the one named last changes fastest.
Arguments:
- state_ens: bfloat16 [512, 131072], P('mem', 'grp'), may hold values from -6 to 6
- obs_ens: bfloat16 [512, 262144], P('mem', 'grp'), may hold values from -6 to 6
- obs_value: float32 [262144], P(('grp', 'mem')), may hold values from -12 to 12
- obs_class: int32 [262144], P(('grp', 'mem')), may hold values from 0 to 15
- loc_table: bfloat16 [16], replicated, may hold values from 0.049804688 to 1
- nbr_weight: float32 [4], replicated, may hold values from 0.25 to 1
Outputs:
- analysis: bfloat16 [512, 131072], P('mem', 'grp')
The draws below stay inside these ranges and needn't reach their ends.
All inputs are finite; a program needn't handle non-finite values.
Results may differ from the reference program's by a relative error of at most 0.0065.
Values may be sent and summed in bfloat16 or wider, within the bound.
No kernel may reach another device: no remote copies, remote signals or barrier semaphores. Data moves between devices by JAX's collectives and lax.ppermute only.
A program may use at most 64 MiB of HBM per device.

```python
import math
import jax
import jax.numpy as jnp
from jax import lax

MEMBERS = 512
CELLS = 512
LOCAL_OBS = 1024
SWEEPS = 5
ROW_PATCHES = 8
CLASSES = 16
ALL_CELLS = 131072
ALL_OBS = 262144
N_GRP = 2
N_MEM = 128


def with_ends(array, rng, least, largest):
    extent = array.shape
    index_at = [jax.random.randint(jax.random.fold_in(rng, axis), (), 0, extent[axis]) for axis in range(len(extent))]
    array = array.at[tuple(index_at)].set(least)
    longest = extent.index(max(extent))
    index_at[longest] = (index_at[longest] + 1) % extent[longest]
    return array.at[tuple(index_at)].set(largest)


def steps_of(rng, extent, cuts, least, top_value):
    def one(axis_at, blocks):
        steps = jax.random.uniform(jax.random.fold_in(jax.random.fold_in(rng, 6), axis_at), (blocks,), jnp.float32, least / len(cuts), top_value / len(cuts))
        return jnp.repeat(jnp.exp(steps), extent[axis_at] // blocks).reshape((-1,) + (1,) * (len(extent) - axis_at - 1))

    level = one(*cuts[0])
    for cut in cuts[1:]:
        level = level * one(*cut)
    return level


def centred(key, shape, scale, limit, split=(), held_as=jnp.bfloat16):
    drawn = scale * jax.random.normal(key, shape, jnp.float32)
    if split:
        drawn = drawn * steps_of(key, shape, split, -0.22, 0.18)
    return jnp.clip(drawn, -limit, limit).astype(held_as)


def setup_inputs(seed: int = 0) -> dict:
    arg_keys = jax.random.split(jax.random.key(seed), 7)
    return {
        "state_ens": centred(arg_keys[0], (MEMBERS, ALL_CELLS), 1.0, 6.0, ((0, 128), (1, 2))),
        "obs_ens": centred(arg_keys[1], (MEMBERS, ALL_OBS), 1.0, 6.0, ((0, 128), (1, 2))),
        "obs_value": centred(arg_keys[2], (ALL_OBS,), 2.0, 12.0, ((0, 256),), jnp.float32),
        "obs_class": with_ends(jax.random.randint(arg_keys[3], (ALL_OBS,), 0, CLASSES), jax.random.fold_in(arg_keys[3], 1), 0, CLASSES - 1).astype(jnp.int32),
        "loc_table": jnp.clip(jnp.exp(jax.random.uniform(arg_keys[4], (CLASSES,), jnp.float32, math.log(0.049804688), math.log(1.0))), 0.049804688, 1.0).astype(jnp.bfloat16),
        "nbr_weight": jnp.clip(jax.random.uniform(arg_keys[5], (4,), jnp.float32, 0.25, 1.0), 0.25, 1.0),
    }


def mirror(product):
    return jnp.triu(product) + jnp.triu(product, 1).T

def newton_root(system):
    norm_total = jnp.sqrt(jnp.sum(system * system))
    identity = jnp.eye(system.shape[0], dtype=jnp.float32)
    iterate = system / norm_total
    root_inv = identity
    for sweep in range(SWEEPS):
        middle = 1.5 * identity - 0.5 * jnp.dot(root_inv, iterate, precision=lax.Precision.HIGHEST)
        iterate = jnp.dot(iterate, middle, precision=lax.Precision.HIGHEST)
        root_inv = jnp.dot(middle, root_inv, precision=lax.Precision.HIGHEST)
    return (root_inv, norm_total)

def reference(state_ens, obs_ens, obs_value, obs_class, loc_table, nbr_weight):
    patches = N_GRP * N_MEM

    def own_terms(index):
        start = (index * LOCAL_OBS).astype(jnp.int32)
        obs_block = lax.dynamic_slice_in_dim(obs_ens, start, LOCAL_OBS, 1)
        observed = lax.dynamic_slice_in_dim(obs_value, start, LOCAL_OBS, 0)
        classes = lax.dynamic_slice_in_dim(obs_class, start, LOCAL_OBS, 0)
        centre = lax.optimization_barrier(jnp.sum(obs_block, axis=0, dtype=jnp.float32)) / MEMBERS
        spread = (obs_block.astype(jnp.float32) - centre).astype(jnp.bfloat16)
        rates = loc_table[classes]
        scaled = (spread.astype(jnp.float32) * rates.astype(jnp.float32)).astype(jnp.bfloat16)
        innovation = (rates.astype(jnp.float32) * (observed - centre)).astype(jnp.bfloat16)
        gram_own = mirror(jnp.dot(spread, scaled.T, preferred_element_type=jnp.float32))
        vector_own = jnp.dot(spread, innovation, preferred_element_type=jnp.float32)
        return (gram_own, vector_own)
    grams, vectors = lax.map(own_terms, jnp.arange(patches, dtype=jnp.int32))

    def analyse(index):
        column = index % ROW_PATCHES
        system = grams[index] + (MEMBERS - 1.0) * jnp.eye(MEMBERS, dtype=jnp.float32)
        rhs_vector = vectors[index]
        links = ((1, 0, column != 0), (-1, 1, column != ROW_PATCHES - 1), (ROW_PATCHES, 2, column >= 0), (-ROW_PATCHES, 3, column >= 0))
        for offset, direction, active in links:
            source = index - offset
            inside = jnp.logical_and(jnp.logical_and(source >= 0, source < patches), active)
            clipped = jnp.clip(source, 0, patches - 1).astype(jnp.int32)
            factor = nbr_weight[direction] * inside.astype(jnp.float32)
            system = system + factor * grams[clipped]
            rhs_vector = rhs_vector + factor * vectors[clipped]
        root_inv, norm_total = newton_root(system)
        half_step = jnp.dot(root_inv, rhs_vector, precision=lax.Precision.HIGHEST)
        mean_weight = jnp.dot(root_inv, half_step, precision=lax.Precision.HIGHEST) / norm_total
        transform = (jnp.sqrt((MEMBERS - 1.0) / norm_total) * root_inv + mean_weight[:, None]).astype(jnp.bfloat16)
        start = (index * CELLS).astype(jnp.int32)
        states = lax.dynamic_slice_in_dim(state_ens, start, CELLS, 1)
        centre = lax.optimization_barrier(jnp.sum(states, axis=0, dtype=jnp.float32)) / MEMBERS
        deviation = (states.astype(jnp.float32) - centre).astype(jnp.bfloat16)
        update = lax.dot_general(transform, deviation, (((0,), (0,)), ((), ())), preferred_element_type=jnp.float32)
        return (centre + update).astype(jnp.bfloat16)
    blocks = lax.map(analyse, jnp.arange(patches, dtype=jnp.int32))
    return jnp.transpose(blocks, (1, 0, 2)).reshape(MEMBERS, patches * CELLS)
```

```python
import jax
import jax.numpy as jnp
from jax import lax
from jax.experimental import pallas as pl
from jax.experimental.pallas import tpu as pltpu
from jax.sharding import PartitionSpec as P

MEMBERS = 512
SWEEPS = 5
ROW_PATCHES = 8
HALF = MEMBERS // 2
VEC = 16
FIRST = MEMBERS + VEC
PACKED = FIRST + HALF + VEC
F32 = jnp.float32
BF16 = jnp.bfloat16


def placement():
    order = []
    for row in range(16):
        z, step = row // 4, row % 4
        x = step if z % 2 == 0 else 3 - step
        order += [x * 32 + z * 8 + w for w in range(ROW_PATCHES)]
    return order


ORDER = placement()


def device_of(patch):
    return patch // 128 * 128 + ORDER[patch % 128]


def links(by):
    pairs = []
    for p in range(256):
        q = p + by
        if 0 <= q < 256 and (abs(by) == ROW_PATCHES or p // ROW_PATCHES == q // ROW_PATCHES):
            pairs.append((device_of(p), device_of(q)))
    return pairs


def lookup(classes, weight_table):
    codes = lax.broadcasted_iota(jnp.int32, (weight_table.shape[0], classes.shape[0]), 0)
    picked = jnp.where(codes == classes[None, :], weight_table.astype(F32)[:, None], 0.0)
    return jnp.sum(picked, axis=0)


def member_sum(ref):
    def step(i, acc):
        return acc + jnp.sum(ref[pl.ds(i * 4, 4)].astype(F32), axis=(0, 1))

    acc = lax.fori_loop(0, 16, step, jnp.zeros((4, ref.shape[3]), F32))
    return jnp.sum(acc, axis=0, keepdims=True)


def rows_of(ref, i):
    block = ref[pl.ds(i * 4, 4)].astype(F32)
    return jnp.concatenate([block[:, 0], block[:, 1]], axis=1).reshape(32, ref.shape[3])


def gram_kernel(obs_ref, val_ref, own_ref, send_ref, spread_ref, left_ref):
    centre = member_sum(obs_ref) / MEMBERS
    observed = val_ref[0:1]
    rates = val_ref[1:2]

    def step(i, carry):
        spread = (rows_of(obs_ref, i) - centre).astype(BF16)
        at = pl.ds(pl.multiple_of(i * 32, 32), 32)
        spread_ref[at] = spread
        left_ref[at] = (spread.astype(F32) * rates).astype(BF16)
        return carry

    lax.fori_loop(0, 16, step, 0)
    innovation = (rates * (observed - centre)).astype(BF16)
    left_ref[pl.ds(MEMBERS, VEC)] = jnp.broadcast_to(innovation, (VEC, innovation.shape[1]))
    contract = (((1,), (1,)), ((), ()))
    is_first = lax.broadcasted_iota(jnp.int32, (VEC, HALF), 0) < 8
    for start, rows, at in ((0, FIRST, 0), (HALF, FIRST - HALF, FIRST)):
        part = lax.dot_general(
            left_ref[pl.ds(start, rows)],
            spread_ref[pl.ds(start, HALF)],
            contract,
            preferred_element_type=F32,
        )
        body = rows - VEC
        own_ref[pl.ds(at, body)] = part[:body]
        send_ref[pl.ds(at, body)] = part[:body].astype(BF16)
        vec = part[body:]
        high = vec.astype(BF16)
        low = (vec - high.astype(F32)).astype(BF16)
        own_ref[pl.ds(at + body, VEC)] = jnp.where(is_first, vec, 0.0)
        send_ref[pl.ds(at + body, VEC)] = jnp.where(
            is_first, high.astype(F32), low.astype(F32)
        ).astype(BF16)


def solve_kernel(
    weight_ref, own_ref, west_ref, east_ref, north_ref, south_ref, out_ref,
    sys_ref, t_ref, w_ref, t2_ref, tb_ref, wb_ref, t2b_ref,
):
    def total(start, rows):
        at = pl.ds(start, rows)
        acc = own_ref[at]
        for k, ref in enumerate((west_ref, east_ref, north_ref, south_ref)):
            acc = acc + weight_ref[k] * ref[at].astype(F32)
        return acc

    row = lax.broadcasted_iota(jnp.int32, (HALF, HALF), 0)
    col = lax.broadcasted_iota(jnp.int32, (HALF, HALF), 1)

    def mirrored(block):
        block = jnp.where(row >= col, block, block.T)
        return block + jnp.where(row == col, MEMBERS - 1.0, 0.0)

    sys_ref[0:HALF, 0:HALF] = mirrored(total(0, HALF))
    cross = total(HALF, HALF)
    sys_ref[HALF:MEMBERS, 0:HALF] = cross
    sys_ref[0:HALF, HALF:MEMBERS] = cross.T
    sys_ref[HALF:MEMBERS, HALF:MEMBERS] = mirrored(total(FIRST, HALF))
    vec0 = total(MEMBERS, VEC)
    vec1 = total(FIRST + HALF, VEC)
    rhs = jnp.concatenate([vec0[0:1] + vec0[8:9], vec1[0:1] + vec1[8:9]], axis=1)

    system = sys_ref[...]
    norm = jnp.sqrt(jnp.sum(jnp.sum(system * system, axis=0, keepdims=True), axis=1, keepdims=True))
    t = system / norm
    t_ref[...] = t
    tb_ref[...] = t.astype(BF16)

    def dot(a, b):
        return jnp.dot(a[...], b[...], preferred_element_type=F32)

    scale = 1.0
    for sweep in range(SWEEPS):
        last = sweep == SWEEPS - 1
        if sweep == 0:
            w = -0.5 * t_ref[...]
        else:
            w = 1.5 * w_ref[...] - (0.5 * scale) * t_ref[...] - 0.5 * dot(tb_ref, wb_ref)
        scale *= 1.5
        w_ref[...] = w
        if not last:
            wb_ref[...] = w.astype(BF16)
            t2 = dot(tb_ref, tb_ref)
            t2_ref[...] = t2
            t2b_ref[...] = t2.astype(BF16)
            t = 2.25 * t_ref[...] - 1.5 * t2_ref[...] + 0.25 * dot(t2b_ref, tb_ref)
            t_ref[...] = t
            tb_ref[...] = t.astype(BF16)

    row = lax.broadcasted_iota(jnp.int32, (MEMBERS, MEMBERS), 0)
    col = lax.broadcasted_iota(jnp.int32, (MEMBERS, MEMBERS), 1)
    root_inv = w_ref[...] + jnp.where(row == col, scale, 0.0)
    half_step = jnp.sum(root_inv * rhs, axis=1, keepdims=True)
    mean_weight = jnp.sum(root_inv * half_step, axis=0, keepdims=True) / norm
    out_ref[...] = (jnp.sqrt((MEMBERS - 1.0) / norm) * root_inv + mean_weight).astype(BF16)


def update_kernel(transform_ref, state_ref, out_ref, dev_ref):
    centre = member_sum(state_ref) / MEMBERS

    def step(i, carry):
        at = pl.ds(pl.multiple_of(i * 32, 32), 32)
        dev_ref[at] = (rows_of(state_ref, i) - centre).astype(BF16)
        return carry

    lax.fori_loop(0, 16, step, 0)
    update = jnp.dot(transform_ref[...], dev_ref[...], preferred_element_type=F32)
    analysis = (centre + update).reshape(64, 8, centre.shape[1])
    out_ref[:, 0] = analysis[:, 0:4].astype(BF16)
    out_ref[:, 1] = analysis[:, 4:8].astype(BF16)


VMEM = pl.BlockSpec(memory_space=pltpu.VMEM)
SMEM = pl.BlockSpec(memory_space=pltpu.SMEM)


def to_patches(array, columns):
    pieces = lax.all_to_all(
        array.reshape(4, 128, columns), "mem", split_axis=1, concat_axis=0, tiled=False,
        axis_index_groups=[ORDER],
    )
    return pieces.reshape(64, 2, 4, columns)


def shards(state_ens, obs_ens, obs_value, obs_class, loc_table, nbr_weight):
    obs = to_patches(obs_ens, 1024)
    values = jnp.stack([obs_value, lookup(obs_class, loc_table)])
    values = lax.ppermute(values, ("grp", "mem"), [(p, device_of(p)) for p in range(256)])
    state_ens, obs, values = lax.optimization_barrier((state_ens, obs, values))
    state = to_patches(state_ens, 512)
    own, send = pl.pallas_call(
        gram_kernel,
        out_shape=(
            jax.ShapeDtypeStruct((PACKED, HALF), F32),
            jax.ShapeDtypeStruct((PACKED, HALF), BF16),
        ),
        in_specs=[VMEM, VMEM],
        out_specs=(VMEM, VMEM),
        scratch_shapes=[pltpu.VMEM((MEMBERS, 1024), BF16), pltpu.VMEM((FIRST, 1024), BF16)],
        name="gram",
    )(obs, values)
    north, south = (lax.ppermute(send, ("grp", "mem"), links(by)) for by in (8, -8))
    west, east = (lax.ppermute(send, ("grp", "mem"), links(by)) for by in (1, -1))
    square = (MEMBERS, MEMBERS)
    transform = pl.pallas_call(
        solve_kernel,
        out_shape=jax.ShapeDtypeStruct(square, BF16),
        in_specs=[SMEM] + [VMEM] * 5,
        out_specs=VMEM,
        scratch_shapes=[pltpu.VMEM(square, F32)] * 4 + [pltpu.VMEM(square, BF16)] * 3,
        name="solve",
    )(nbr_weight, own, west, east, north, south)
    analysis = pl.pallas_call(
        update_kernel,
        out_shape=jax.ShapeDtypeStruct((64, 2, 4, 512), BF16),
        in_specs=[VMEM, VMEM],
        out_specs=VMEM,
        scratch_shapes=[pltpu.VMEM(square, BF16)],
        name="update",
    )(transform, state)
    back = lax.all_to_all(
        analysis.reshape(128, 4, 512), "mem", split_axis=0, concat_axis=1, tiled=False,
        axis_index_groups=[ORDER],
    )
    return back.reshape(4, 65536)


def solution(mesh):
    in_specs = (P("mem", "grp"), P("mem", "grp"), P(("grp", "mem")), P(("grp", "mem")), P(), P())
    out_specs = P("mem", "grp")
    return jax.shard_map(shards, mesh=mesh, in_specs=in_specs, out_specs=out_specs, check_vma=False)
```

```python
import jax
import jax.numpy as jnp
from jax import lax
from jax.experimental import pallas as pl
from jax.experimental.pallas import tpu as pltpu
from jax.sharding import PartitionSpec as P

MEMBERS = 512
SWEEPS = 5
CELLS = 512
LOCAL_OBS = 1024
ROW_PATCHES = 8
HALF = MEMBERS // 2
QUARTER = MEMBERS // 4
VEC = 16
TAIL = MEMBERS + QUARTER
PACKED = TAIL + VEC
F32 = jnp.float32
BF16 = jnp.bfloat16


def placement():
    order = []
    for row in range(16):
        z, step = row // 4, row % 4
        x = step if z % 2 == 0 else 3 - step
        order += [x * 32 + z * 8 + w for w in range(ROW_PATCHES)]
    return order


ORDER = placement()


def device_of(patch):
    return patch // 128 * 128 + ORDER[patch % 128]


def swaps(by, parity):
    pairs = []
    for p in range(256):
        row, column = p // ROW_PATCHES, p % ROW_PATCHES
        q = p + by
        if q < 256 and (by == ROW_PATCHES or q // ROW_PATCHES == row):
            if (row if by == ROW_PATCHES else column) % 2 == parity:
                pairs += [(device_of(p), device_of(q)), (device_of(q), device_of(p))]
    return pairs


def swap_weights(weight_ref):
    west, east, north, south = (weight_ref[k] for k in range(4))
    mem = lax.axis_index("mem")
    even_row = lax.rem(lax.div(mem, 32) + lax.div(mem, 8), 2) == 0
    even_column = lax.rem(mem, 2) == 0
    return (
        jnp.where(even_row, south, north),
        jnp.where(even_row, north, south),
        jnp.where(even_column, west, east),
        jnp.where(even_column, east, west),
    )


def lookup(classes, weight_table):
    codes = lax.broadcasted_iota(jnp.int32, (weight_table.shape[0], classes.shape[0]), 0)
    picked = jnp.where(codes == classes[None, :], weight_table.astype(F32)[:, None], 0.0)
    return jnp.sum(picked, axis=0)


def join_kernel(obs_ref, state_ref, out_ref, sem):
    copies = [
        pltpu.make_async_copy(obs_ref, out_ref.at[:, :, pl.ds(0, LOCAL_OBS)], sem.at[0]),
        pltpu.make_async_copy(state_ref, out_ref.at[:, :, pl.ds(LOCAL_OBS, CELLS)], sem.at[1]),
    ]
    for copy in copies:
        copy.start()
    for copy in copies:
        copy.wait()


def gather_rows(ref, columns, rows_ref):
    width = rows_ref.shape[1]

    def step(i, acc):
        block = ref[pl.ds(i * 4, 4), :, :, columns].astype(F32)
        block = jnp.concatenate([block[:, 0], block[:, 1]], axis=1)
        rows_ref[pl.ds(pl.multiple_of(i * 32, 32), 32)] = block.reshape(32, width).astype(BF16)
        return acc + jnp.sum(block, axis=0)

    acc = lax.fori_loop(0, 16, step, jnp.zeros((8, width), F32))
    return jnp.sum(acc, axis=0, keepdims=True) / MEMBERS


def gram_kernel(obs_ref, val_ref, own_ref, send_ref, spread_ref, left_ref):
    centre = gather_rows(obs_ref, pl.ds(0, LOCAL_OBS), spread_ref)
    observed = val_ref[0:1]
    rates = val_ref[1:2]

    def step(i, carry):
        at = pl.ds(pl.multiple_of(i * 32, 32), 32)
        spread = (spread_ref[at].astype(F32) - centre).astype(BF16)
        spread_ref[at] = spread
        left_ref[at] = (spread.astype(F32) * rates).astype(BF16)
        return carry

    lax.fori_loop(0, 16, step, 0)
    innovation = (rates * (observed - centre)).astype(BF16)
    left_ref[pl.ds(MEMBERS, VEC)] = jnp.broadcast_to(innovation, (VEC, innovation.shape[1]))
    contract = (((1,), (1,)), ((), ()))
    first = lax.dot_general(
        left_ref[...], spread_ref[0:HALF], contract, preferred_element_type=F32
    )
    second = lax.dot_general(
        left_ref[HALF:], spread_ref[HALF:MEMBERS], contract, preferred_element_type=F32
    )
    for at, part in (
        ((slice(0, QUARTER), slice(0, QUARTER)), first[0:QUARTER, 0:QUARTER]),
        ((slice(0, QUARTER), slice(QUARTER, HALF)), second[0:QUARTER, 0:QUARTER]),
        ((slice(QUARTER, MEMBERS), slice(0, HALF)), first[QUARTER:MEMBERS]),
        ((slice(MEMBERS, TAIL), slice(0, HALF)), second[QUARTER:HALF]),
    ):
        own_ref[at] = part
        send_ref[at] = part.astype(BF16)
    row = lax.broadcasted_iota(jnp.int32, (VEC, HALF), 0)
    vec = jnp.where(row < 8, first[MEMBERS:], second[HALF:])
    high = vec.astype(BF16).astype(F32)
    is_high = row % 8 < 4
    own_ref[TAIL:PACKED] = jnp.where(is_high, vec, 0.0)
    send_ref[TAIL:PACKED] = jnp.where(is_high, high, vec - high).astype(BF16)


def solve_kernel(
    weight_ref, own_ref, ns0_ref, ns1_ref, ew1_ref, ew0_ref, dev_ref, centre_ref, out_ref,
    sys_ref, t_ref, w_ref, t2_ref, tb_ref, wb_ref, t2b_ref,
):
    weights = swap_weights(weight_ref)

    def total(start, rows):
        at = pl.ds(start, rows)
        acc = own_ref[at]
        for k, ref in enumerate((ns0_ref, ns1_ref, ew1_ref, ew0_ref)):
            acc = acc + weights[k] * ref[at].astype(F32)
        return acc

    row = lax.broadcasted_iota(jnp.int32, (QUARTER, QUARTER), 0)
    col = lax.broadcasted_iota(jnp.int32, (QUARTER, QUARTER), 1)

    def diagonal(block):
        block = jnp.where(row >= col, block, block.T)
        return block + jnp.where(row == col, MEMBERS - 1.0, 0.0)

    top = total(0, QUARTER)
    for start, left, at in ((0, 0, QUARTER), (HALF, QUARTER, MEMBERS)):
        a, b, c = start, start + QUARTER, start + HALF
        low = total(at, QUARTER)
        sys_ref[a:b, a:b] = diagonal(top[:, left:left + QUARTER])
        sys_ref[b:c, a:b] = low[:, 0:QUARTER]
        sys_ref[a:b, b:c] = low[:, 0:QUARTER].T
        sys_ref[b:c, b:c] = diagonal(low[:, QUARTER:])
    cross = total(HALF, HALF)
    sys_ref[HALF:MEMBERS, 0:HALF] = cross
    sys_ref[0:HALF, HALF:MEMBERS] = cross.T
    vec = total(TAIL, VEC)
    rhs = jnp.concatenate([vec[0:1] + vec[4:5], vec[8:9] + vec[12:13]], axis=1)

    system = sys_ref[...]
    norm = jnp.sqrt(jnp.sum(jnp.sum(system * system, axis=0, keepdims=True), axis=1, keepdims=True))
    t = system / norm
    t_ref[...] = t
    tb_ref[...] = t.astype(BF16)

    def dot(a, b):
        return jnp.dot(a[...], b[...], preferred_element_type=F32)

    scale = 1.0
    for sweep in range(SWEEPS):
        last = sweep == SWEEPS - 1
        if sweep == 0:
            w = -0.5 * t_ref[...]
        else:
            w = 1.5 * w_ref[...] - (0.5 * scale) * t_ref[...] - 0.5 * dot(tb_ref, wb_ref)
        scale *= 1.5
        w_ref[...] = w
        if not last:
            wb_ref[...] = w.astype(BF16)
            t2 = dot(tb_ref, tb_ref)
            t2_ref[...] = t2
            t2b_ref[...] = t2.astype(BF16)
            t = 2.25 * t_ref[...] - 1.5 * t2_ref[...] + 0.25 * dot(t2b_ref, tb_ref)
            t_ref[...] = t
            tb_ref[...] = t.astype(BF16)

    row = lax.broadcasted_iota(jnp.int32, (MEMBERS, MEMBERS), 0)
    col = lax.broadcasted_iota(jnp.int32, (MEMBERS, MEMBERS), 1)
    root_inv = w_ref[...] + jnp.where(row == col, scale, 0.0)
    half_step = jnp.sum(root_inv * rhs, axis=1, keepdims=True)
    mean_weight = jnp.sum(root_inv * half_step, axis=0, keepdims=True) / norm
    tb_ref[...] = (jnp.sqrt((MEMBERS - 1.0) / norm) * root_inv + mean_weight).astype(BF16)
    analysis = (centre_ref[...] + dot(tb_ref, dev_ref)).reshape(64, 8, CELLS)
    out_ref[:, 0] = analysis[:, 0:4].astype(BF16)
    out_ref[:, 1] = analysis[:, 4:8].astype(BF16)


def state_kernel(state_ref, dev_ref, centre_ref):
    centre = gather_rows(state_ref, pl.ds(LOCAL_OBS, CELLS), dev_ref)
    centre_ref[...] = centre

    def step(i, carry):
        at = pl.ds(pl.multiple_of(i * 32, 32), 32)
        dev_ref[at] = (dev_ref[at].astype(F32) - centre).astype(BF16)
        return carry

    lax.fori_loop(0, 16, step, 0)


def vmem(mebibytes):
    return pltpu.CompilerParams(vmem_limit_bytes=mebibytes * 2**20)


VMEM = pl.BlockSpec(memory_space=pltpu.VMEM)
HBM = pl.BlockSpec(memory_space=pltpu.HBM)
SMEM = pl.BlockSpec(memory_space=pltpu.SMEM)


def in_hbm(array):
    return pltpu.with_memory_space_constraint(array, pltpu.HBM)


def shards(state_ens, obs_ens, obs_value, obs_class, loc_table, nbr_weight):
    columns = LOCAL_OBS + CELLS
    both = pl.pallas_call(
        join_kernel,
        out_shape=pltpu.VMEM((128, 4, columns), BF16),
        in_specs=[HBM, HBM],
        out_specs=VMEM,
        scratch_shapes=[pltpu.SemaphoreType.DMA((2,))],
        compiler_params=vmem(2),
        name="join",
    )(
        in_hbm(obs_ens.reshape(4, 128, LOCAL_OBS).transpose(1, 0, 2)),
        in_hbm(state_ens.reshape(4, 128, CELLS).transpose(1, 0, 2)),
    )
    both = lax.all_to_all(
        both, "mem", split_axis=0, concat_axis=0, tiled=False, axis_index_groups=[ORDER]
    ).reshape(64, 2, 4, columns)
    values = jnp.stack([obs_value, lookup(obs_class, loc_table)])
    values = lax.ppermute(values, ("grp", "mem"), [(p, device_of(p)) for p in range(256)])
    own, send = pl.pallas_call(
        gram_kernel,
        out_shape=(
            pltpu.VMEM((PACKED, HALF), F32),
            pltpu.VMEM((PACKED, HALF), BF16),
        ),
        in_specs=[VMEM, VMEM],
        out_specs=(VMEM, VMEM),
        scratch_shapes=[pltpu.VMEM((MEMBERS, LOCAL_OBS), BF16), pltpu.VMEM((MEMBERS + VEC, LOCAL_OBS), BF16)],
        compiler_params=vmem(10),
        name="gram",
    )(both, values)
    received = [
        lax.ppermute(send, ("grp", "mem"), swaps(by, parity))
        for by, parity in ((ROW_PATCHES, 0), (ROW_PATCHES, 1), (1, 1), (1, 0))
    ]
    both, own = lax.optimization_barrier((both, own))
    deviation, centre = pl.pallas_call(
        state_kernel,
        out_shape=(
            jax.ShapeDtypeStruct((MEMBERS, CELLS), BF16),
            jax.ShapeDtypeStruct((1, CELLS), F32),
        ),
        in_specs=[VMEM],
        out_specs=(VMEM, VMEM),
        cost_estimate=pl.CostEstimate(flops=2**20, bytes_accessed=2**21, transcendentals=0),
        compiler_params=vmem(4),
        name="state",
    )(both)
    square = (MEMBERS, MEMBERS)
    analysis = pl.pallas_call(
        solve_kernel,
        out_shape=jax.ShapeDtypeStruct((64, 2, 4, CELLS), BF16),
        in_specs=[SMEM] + [VMEM] * 7,
        out_specs=VMEM,
        scratch_shapes=[pltpu.VMEM(square, F32)] * 4 + [pltpu.VMEM(square, BF16)] * 3,
        compiler_params=vmem(16),
        name="solve",
    )(nbr_weight, own, *received, deviation, centre)
    back = lax.all_to_all(
        analysis.reshape(128, 4, CELLS), "mem", split_axis=0, concat_axis=1, tiled=False,
        axis_index_groups=[ORDER],
    )
    return back.reshape(4, 65536)


def solution(mesh):
    in_specs = (P("mem", "grp"), P("mem", "grp"), P(("grp", "mem")), P(("grp", "mem")), P(), P())
    out_specs = P("mem", "grp")
    return jax.shard_map(shards, mesh=mesh, in_specs=in_specs, out_specs=out_specs, check_vma=False)
```

```python
import jax
import jax.numpy as jnp
from jax import lax
from jax.experimental import pallas as pl
from jax.experimental.pallas import tpu as pltpu
from jax.sharding import PartitionSpec as P

MEMBERS = 512
CELLS = 512
LOCAL_OBS = 1024
JOINED = 16
STORES = 4
ROW_PATCHES = 8
HALF = MEMBERS // 2
QUARTER = MEMBERS // 4
VEC = 16
PACKED = MEMBERS + VEC
F32 = jnp.float32
BF16 = jnp.bfloat16


def placement():
    order = []
    for row in range(16):
        z, step = row // 4, row % 4
        x = 3 - step if z % 2 == 0 else step
        order += [x * 32 + z * 8 + w for w in range(ROW_PATCHES)]
    return order


ORDER = placement()


def device_of(patch):
    return patch // 128 * 128 + ORDER[patch % 128]


def swaps(by, parity):
    pairs = []
    for p in range(256):
        row, column = p // ROW_PATCHES, p % ROW_PATCHES
        q = p + by
        if q < 256 and (by == ROW_PATCHES or q // ROW_PATCHES == row):
            if (row if by == ROW_PATCHES else column) % 2 == parity:
                pairs += [(device_of(p), device_of(q)), (device_of(q), device_of(p))]
    return pairs


def swap_weights(weight_ref):
    west, east, north, south = (weight_ref[k] for k in range(4))
    mem = lax.axis_index("mem")
    even_row = lax.rem(lax.div(mem, 32) + lax.div(mem, 8), 2) == 1
    even_column = lax.rem(mem, 2) == 0
    return (
        jnp.where(even_row, south, north),
        jnp.where(even_row, north, south),
        jnp.where(even_column, west, east),
        jnp.where(even_column, east, west),
    )


def lookup(classes, weight_table):
    codes = lax.broadcasted_iota(jnp.int32, (weight_table.shape[0], classes.shape[0]), 0)
    picked = jnp.where(codes == classes[None, :], weight_table.astype(F32)[:, None], 0.0)
    return jnp.sum(picked, axis=0)


def join_kernel(obs_ref, state_ref, out_ref, both_ref, in_sem, out_sem):
    def chunk(k):
        return pl.ds(k * JOINED, JOINED)

    def fetch(k):
        at = chunk(k)
        return (
            pltpu.make_async_copy(
                obs_ref.at[at], both_ref.at[at, :, pl.ds(0, LOCAL_OBS)], in_sem.at[0, k]
            ),
            pltpu.make_async_copy(
                state_ref.at[at], both_ref.at[at, :, pl.ds(LOCAL_OBS, CELLS)], in_sem.at[1, k]
            ),
        )

    def put(k):
        return pltpu.make_async_copy(both_ref.at[chunk(k)], out_ref.at[chunk(k)], out_sem.at[k])

    for k in range(128 // JOINED):
        for copy in fetch(k):
            copy.start()
    for k in range(128 // JOINED):
        for copy in fetch(k):
            copy.wait()
        put(k).start()
    for k in range(128 // JOINED):
        put(k).wait()


def gather_rows(ref, columns, rows_ref):
    width = rows_ref.shape[1]

    def step(i, acc):
        block = ref[pl.ds(i * 4, 4), :, :, columns].astype(F32)
        block = jnp.concatenate([block[:, 0], block[:, 1]], axis=1)
        rows_ref[pl.ds(pl.multiple_of(i * 32, 32), 32)] = block.reshape(32, width).astype(BF16)
        return acc + jnp.sum(block, axis=0)

    acc = lax.fori_loop(0, 16, step, jnp.zeros((8, width), F32))
    return jnp.sum(acc, axis=0, keepdims=True) / MEMBERS


def gram_kernel(obs_ref, val_ref, own_ref, send_ref, spread_ref, left_ref):
    centre = gather_rows(obs_ref, pl.ds(0, LOCAL_OBS), spread_ref)
    observed = val_ref[0:1]
    rates = val_ref[1:2]

    def step(i, carry):
        at = pl.ds(pl.multiple_of(i * 32, 32), 32)
        spread = (spread_ref[at].astype(F32) - centre).astype(BF16)
        spread_ref[at] = spread
        left_ref[at] = (spread.astype(F32) * rates).astype(BF16)
        return carry

    lax.fori_loop(0, 16, step, 0)
    innovation = (rates * (observed - centre)).astype(BF16)
    left_ref[pl.ds(MEMBERS, VEC)] = jnp.broadcast_to(innovation, (VEC, innovation.shape[1]))
    contract = (((1,), (1,)), ((), ()))
    first = lax.dot_general(
        left_ref[...], spread_ref[0:HALF], contract, preferred_element_type=F32
    )
    second = lax.dot_general(
        left_ref[HALF:], spread_ref[HALF:MEMBERS], contract, preferred_element_type=F32
    )
    row = lax.broadcasted_iota(jnp.int32, (QUARTER, QUARTER), 0)
    col = lax.broadcasted_iota(jnp.int32, (QUARTER, QUARTER), 1)

    def put(rows, columns, part):
        own_ref[rows, columns] = part
        send_ref[rows, columns] = part.astype(BF16)

    low, high = slice(0, QUARTER), slice(QUARTER, HALF)
    diagonals = []
    for part, columns in ((first, low), (second, high)):
        last = part[high, high]
        put(low, columns, jnp.where(row >= col, part[low, low], last.T))
        put(high, columns, part[high, low])
        diagonals.append(jnp.sum(jnp.where(row == col, last, 0.0), axis=0, keepdims=True))
    put(slice(HALF, MEMBERS), slice(0, HALF), first[HALF:MEMBERS])
    row = lax.broadcasted_iota(jnp.int32, (VEC, HALF), 0)
    tail = jnp.where(row < 8, first[MEMBERS:], second[HALF:])
    tail = jnp.where(row % 4 == 2, jnp.concatenate(diagonals, axis=1), tail)
    rounded = tail.astype(BF16).astype(F32)
    is_high = row % 8 < 4
    own_ref[MEMBERS:] = jnp.where(is_high, tail, 0.0)
    send_ref[MEMBERS:] = jnp.where(is_high, rounded, tail - rounded).astype(BF16)


def solve_kernel(
    weight_ref, own_ref, ns0_ref, ns1_ref, ew1_ref, ew0_ref, dev_ref, centre_ref, out_ref,
    sys_ref, t_ref, w_ref, w2_ref, tb_ref, wb_ref, w2b_ref, sb_ref, ub_ref,
):
    weights = swap_weights(weight_ref)

    def total(start, rows):
        at = pl.ds(start, rows)
        acc = own_ref[at]
        for k, ref in enumerate((ns0_ref, ns1_ref, ew1_ref, ew0_ref)):
            acc = acc + weights[k] * ref[at].astype(F32)
        return acc

    row = lax.broadcasted_iota(jnp.int32, (QUARTER, QUARTER), 0)
    col = lax.broadcasted_iota(jnp.int32, (QUARTER, QUARTER), 1)

    top, low, tail = total(0, QUARTER), total(QUARTER, QUARTER), total(MEMBERS, VEC)
    inflation = jnp.where(row == col, MEMBERS - 1.0, 0.0)
    diagonals = tail[2:3] + tail[6:7]
    for start, columns in ((0, slice(0, QUARTER)), (HALF, slice(QUARTER, HALF))):
        a, b, c = start, start + QUARTER, start + HALF
        square, cross = top[:, columns], low[:, columns]
        turned = square.T
        sys_ref[a:b, a:b] = jnp.where(row >= col, square, turned) + inflation
        square = jnp.where(row < col, square, turned)
        sys_ref[b:c, b:c] = jnp.where(row == col, diagonals[:, columns], square) + inflation
        sys_ref[b:c, a:b] = cross
        sys_ref[a:b, b:c] = cross.T
    cross = total(HALF, HALF)
    sys_ref[HALF:MEMBERS, 0:HALF] = cross
    sys_ref[0:HALF, HALF:MEMBERS] = cross.T
    rhs = jnp.concatenate([tail[0:1] + tail[4:5], tail[8:9] + tail[12:13]], axis=1)

    system = sys_ref[...]
    squares = jnp.sum(jnp.sum(system * system, axis=0, keepdims=True), axis=1, keepdims=True)
    norm = jnp.sqrt(squares)

    def dot(a, b):
        return jnp.dot(a[...], b[...], preferred_element_type=F32)

    def two_sweeps(w_ref, wb_ref):
        square = dot(tb_ref, tb_ref)
        sb_ref[...] = square.astype(BF16)
        ub_ref[...] = (0.0625 * square - 0.5625 * t_ref[...]).astype(BF16)
        w_ref[...] = 1.6875 * square - 2.4375 * t_ref[...]
        w = w_ref[...] + dot(ub_ref, sb_ref)
        w_ref[...] = w
        wb_ref[...] = w.astype(BF16)
        ub_ref[...] = (4.5 * w_ref[...] + dot(wb_ref, wb_ref)).astype(BF16)
        t = 5.0625 * t_ref[...] + dot(ub_ref, tb_ref)
        t_ref[...] = t
        tb_ref[...] = t.astype(BF16)

    t = system * (1.0 / norm)
    t_ref[...] = t
    tb_ref[...] = t.astype(BF16)
    two_sweeps(w_ref, wb_ref)
    two_sweeps(w2_ref, w2b_ref)
    w = 2.25 * (w_ref[...] + w2_ref[...]) + dot(wb_ref, w2b_ref)
    w_ref[...] = w
    wb_ref[...] = w.astype(BF16)
    w = 1.5 * w_ref[...] - 2.53125 * t_ref[...] - 0.5 * dot(wb_ref, tb_ref)

    row = lax.broadcasted_iota(jnp.int32, (MEMBERS, MEMBERS), 0)
    col = lax.broadcasted_iota(jnp.int32, (MEMBERS, MEMBERS), 1)
    root_inv = w + jnp.where(row == col, 1.5 * 5.0625, 0.0)
    half_step = jnp.sum(root_inv * rhs, axis=1, keepdims=True)
    mean_weight = jnp.sum(root_inv * half_step, axis=0, keepdims=True) / norm
    tb_ref[...] = (jnp.sqrt((MEMBERS - 1.0) / norm) * root_inv + mean_weight).astype(BF16)
    analysis = (centre_ref[...] + dot(tb_ref, dev_ref)).reshape(64, 8, CELLS)
    out_ref[:, 0] = analysis[:, 0:4].astype(BF16)
    out_ref[:, 1] = analysis[:, 4:8].astype(BF16)


def store_kernel(in_ref, out_ref, sem):
    width = in_ref.shape[1] // STORES
    copies = []
    for k in range(STORES):
        at = pl.ds(k * width, width)
        copies.append(pltpu.make_async_copy(in_ref.at[:, at], out_ref.at[:, at], sem.at[k]))
    for copy in copies:
        copy.start()
    for copy in copies:
        copy.wait()


def state_kernel(state_ref, dev_ref, centre_ref):
    centre = gather_rows(state_ref, pl.ds(LOCAL_OBS, CELLS), dev_ref)
    centre_ref[...] = centre

    def step(i, carry):
        at = pl.ds(pl.multiple_of(i * 32, 32), 32)
        dev_ref[at] = (dev_ref[at].astype(F32) - centre).astype(BF16)
        return carry

    lax.fori_loop(0, 16, step, 0)


def vmem(mebibytes):
    return pltpu.CompilerParams(vmem_limit_bytes=mebibytes * 2**20)


VMEM = pl.BlockSpec(memory_space=pltpu.VMEM)
HBM = pl.BlockSpec(memory_space=pltpu.HBM)
SMEM = pl.BlockSpec(memory_space=pltpu.SMEM)


def in_hbm(array):
    return pltpu.with_memory_space_constraint(array, pltpu.HBM)


def shards(state_ens, obs_ens, obs_value, obs_class, loc_table, nbr_weight):
    columns = LOCAL_OBS + CELLS
    both = pl.pallas_call(
        join_kernel,
        out_shape=jax.ShapeDtypeStruct((128, 4, columns), BF16),
        in_specs=[HBM, HBM],
        out_specs=HBM,
        scratch_shapes=[
            pltpu.VMEM((128, 4, columns), BF16),
            pltpu.SemaphoreType.DMA((2, 128 // JOINED)),
            pltpu.SemaphoreType.DMA((128 // JOINED,)),
        ],
        compiler_params=vmem(4),
        name="join",
    )(
        in_hbm(obs_ens.reshape(4, 128, LOCAL_OBS).transpose(1, 0, 2)),
        in_hbm(state_ens.reshape(4, 128, CELLS).transpose(1, 0, 2)),
    )
    both = lax.all_to_all(
        both, "mem", split_axis=0, concat_axis=0, tiled=False, axis_index_groups=[ORDER]
    ).reshape(64, 2, 4, columns)
    values = jnp.stack([obs_value, lookup(obs_class, loc_table)])
    values = lax.ppermute(values, ("grp", "mem"), [(p, device_of(p)) for p in range(256)])
    own, send = pl.pallas_call(
        gram_kernel,
        out_shape=(
            jax.ShapeDtypeStruct((PACKED, HALF), F32),
            jax.ShapeDtypeStruct((PACKED, HALF), BF16),
        ),
        in_specs=[VMEM, VMEM],
        out_specs=(VMEM, VMEM),
        scratch_shapes=[pltpu.VMEM((MEMBERS, LOCAL_OBS), BF16), pltpu.VMEM((MEMBERS + VEC, LOCAL_OBS), BF16)],
        compiler_params=vmem(10),
        name="gram",
    )(both, values)
    received = [
        lax.ppermute(send, ("grp", "mem"), swaps(by, parity))
        for by, parity in ((ROW_PATCHES, 0), (ROW_PATCHES, 1), (1, 1), (1, 0))
    ]
    both, own = lax.optimization_barrier((both, own))
    deviation, centre = pl.pallas_call(
        state_kernel,
        out_shape=(
            jax.ShapeDtypeStruct((MEMBERS, CELLS), BF16),
            jax.ShapeDtypeStruct((1, CELLS), F32),
        ),
        in_specs=[VMEM],
        out_specs=(VMEM, VMEM),
        cost_estimate=pl.CostEstimate(flops=2**20, bytes_accessed=2**21, transcendentals=0),
        compiler_params=vmem(4),
        name="state",
    )(both)
    square = (MEMBERS, MEMBERS)
    analysis = pl.pallas_call(
        solve_kernel,
        out_shape=jax.ShapeDtypeStruct((64, 2, 4, CELLS), BF16),
        in_specs=[SMEM] + [VMEM] * 7,
        out_specs=VMEM,
        scratch_shapes=[pltpu.VMEM(square, F32)] * 4 + [pltpu.VMEM(square, BF16)] * 5,
        compiler_params=vmem(16),
        name="solve",
    )(nbr_weight, own, *received, deviation, centre)
    back = lax.all_to_all(
        analysis.reshape(128, 4, CELLS), "mem", split_axis=0, concat_axis=1, tiled=False,
        axis_index_groups=[ORDER],
    )
    return pl.pallas_call(
        store_kernel,
        out_shape=jax.ShapeDtypeStruct((4, 65536), BF16),
        in_specs=[VMEM],
        out_specs=HBM,
        scratch_shapes=[pltpu.SemaphoreType.DMA((STORES,))],
        compiler_params=vmem(2),
        name="store",
    )(back.reshape(4, 65536))


def solution(mesh):
    in_specs = (P("mem", "grp"), P("mem", "grp"), P(("grp", "mem")), P(("grp", "mem")), P(), P())
    out_specs = P("mem", "grp")
    return jax.shard_map(shards, mesh=mesh, in_specs=in_specs, out_specs=out_specs, check_vma=False)
```

```python
import jax
import jax.numpy as jnp
from jax import lax
from jax.experimental import pallas as pl
from jax.experimental.pallas import tpu as pltpu
from jax.sharding import PartitionSpec as P


MEMBERS = 512
CELLS = 512
LOCAL_OBS = 1024
ROW_PATCHES = 8
HALF = MEMBERS // 2
QUARTER = MEMBERS // 4
VEC = 16
PACKED = MEMBERS + VEC
F32 = jnp.float32
BF16 = jnp.bfloat16


def placement():
    order = []
    for row in range(16):
        z, step = row // 4, row % 4
        x = 3 - step if z % 2 == 0 else step
        order += [x * 32 + z * 8 + w for w in range(ROW_PATCHES)]
    return order


ORDER = placement()


def device_of(patch):
    return patch // 128 * 128 + ORDER[patch % 128]


def swaps(by, parity):
    pairs = []
    for p in range(256):
        row, column = p // ROW_PATCHES, p % ROW_PATCHES
        q = p + by
        if q < 256 and (by == ROW_PATCHES or q // ROW_PATCHES == row):
            if (row if by == ROW_PATCHES else column) % 2 == parity:
                pairs += [(device_of(p), device_of(q)), (device_of(q), device_of(p))]
    return pairs


def swap_weights(weight_ref):
    west, east, north, south = (weight_ref[k] for k in range(4))
    mem = lax.axis_index("mem")
    even_row = lax.rem(lax.div(mem, 32) + lax.div(mem, 8), 2) == 1
    even_column = lax.rem(mem, 2) == 0
    return (
        jnp.where(even_row, south, north),
        jnp.where(even_row, north, south),
        jnp.where(even_column, west, east),
        jnp.where(even_column, east, west),
    )


def lookup(classes, weight_table):
    codes = lax.broadcasted_iota(jnp.int32, (weight_table.shape[0], classes.shape[0]), 0)
    picked = jnp.where(codes == classes[None, :], weight_table.astype(F32)[:, None], 0.0)
    return jnp.sum(picked, axis=0)


def my_column():
    return lax.rem(lax.axis_index("mem"), ROW_PATCHES)


def split_kernel(state_ref, *rest):
    outs, sem = rest[:ROW_PATCHES], rest[ROW_PATCHES]
    copies = [
        pltpu.make_async_copy(state_ref.at[:, my_column() ^ d], outs[d], sem.at[d])
        for d in range(ROW_PATCHES)
    ]
    for copy in copies:
        copy.start()
    for copy in copies:
        copy.wait()


def merge_kernel(*refs):
    parts, out_ref, sem = refs[:ROW_PATCHES], refs[ROW_PATCHES], refs[ROW_PATCHES + 1]
    copies = [
        pltpu.make_async_copy(parts[d], out_ref.at[:, d], sem.at[d]) for d in range(ROW_PATCHES)
    ]
    for copy in copies:
        copy.start()
    for copy in copies:
        copy.wait()


def gather_rows(ref, rows_ref):
    width = rows_ref.shape[1]

    def step(i, acc):
        block = ref[pl.ds(i * 4, 4)].astype(F32)
        block = jnp.concatenate([block[:, 0], block[:, 1]], axis=1)
        rows_ref[pl.ds(pl.multiple_of(i * 32, 32), 32)] = block.reshape(32, width).astype(BF16)
        return acc + jnp.sum(block, axis=0)

    acc = lax.fori_loop(0, 16, step, jnp.zeros((8, width), F32))
    return jnp.sum(acc, axis=0, keepdims=True) / MEMBERS


def gram_kernel(obs_ref, val_ref, own_ref, send_ref, spread_ref, left_ref):
    centre = gather_rows(obs_ref, spread_ref)
    observed = val_ref[0:1]
    rates = val_ref[1:2]

    def step(i, carry):
        at = pl.ds(pl.multiple_of(i * 32, 32), 32)
        spread = (spread_ref[at].astype(F32) - centre).astype(BF16)
        spread_ref[at] = spread
        left_ref[at] = (spread.astype(F32) * rates).astype(BF16)
        return carry

    lax.fori_loop(0, 16, step, 0)
    innovation = (rates * (observed - centre)).astype(BF16)
    left_ref[pl.ds(MEMBERS, VEC)] = jnp.broadcast_to(innovation, (VEC, innovation.shape[1]))
    contract = (((1,), (1,)), ((), ()))
    first = lax.dot_general(
        left_ref[...], spread_ref[0:HALF], contract, preferred_element_type=F32
    )
    second = lax.dot_general(
        left_ref[HALF:], spread_ref[HALF:MEMBERS], contract, preferred_element_type=F32
    )
    row = lax.broadcasted_iota(jnp.int32, (QUARTER, QUARTER), 0)
    col = lax.broadcasted_iota(jnp.int32, (QUARTER, QUARTER), 1)

    def put(rows, columns, part):
        own_ref[rows, columns] = part
        send_ref[rows, columns] = part.astype(BF16)

    low, high = slice(0, QUARTER), slice(QUARTER, HALF)
    diagonals = []
    for part, columns in ((first, low), (second, high)):
        last = part[high, high]
        put(low, columns, jnp.where(row >= col, part[low, low], last.T))
        put(high, columns, part[high, low])
        diagonals.append(jnp.sum(jnp.where(row == col, last, 0.0), axis=0, keepdims=True))
    put(slice(HALF, MEMBERS), slice(0, HALF), first[HALF:MEMBERS])
    row = lax.broadcasted_iota(jnp.int32, (VEC, HALF), 0)
    tail = jnp.where(row < 8, first[MEMBERS:], second[HALF:])
    tail = jnp.where(row % 4 == 2, jnp.concatenate(diagonals, axis=1), tail)
    rounded = tail.astype(BF16).astype(F32)
    is_high = row % 8 < 4
    own_ref[MEMBERS:] = jnp.where(is_high, tail, 0.0)
    send_ref[MEMBERS:] = jnp.where(is_high, rounded, tail - rounded).astype(BF16)


def solve_kernel(
    weight_ref, own_ref, ns0_ref, ns1_ref, ew1_ref, ew0_ref, out_ref,
    sys_ref, t_ref, w_ref, w2_ref, tb_ref, wb_ref, w2b_ref, sb_ref, ub_ref,
):
    weights = swap_weights(weight_ref)

    def total(start, rows):
        at = pl.ds(start, rows)
        acc = own_ref[at]
        for k, ref in enumerate((ns0_ref, ns1_ref, ew1_ref, ew0_ref)):
            acc = acc + weights[k] * ref[at].astype(F32)
        return acc

    row = lax.broadcasted_iota(jnp.int32, (QUARTER, QUARTER), 0)
    col = lax.broadcasted_iota(jnp.int32, (QUARTER, QUARTER), 1)

    top, low, tail = total(0, QUARTER), total(QUARTER, QUARTER), total(MEMBERS, VEC)
    inflation = jnp.where(row == col, MEMBERS - 1.0, 0.0)
    diagonals = tail[2:3] + tail[6:7]
    for start, columns in ((0, slice(0, QUARTER)), (HALF, slice(QUARTER, HALF))):
        a, b, c = start, start + QUARTER, start + HALF
        square, cross = top[:, columns], low[:, columns]
        turned = square.T
        sys_ref[a:b, a:b] = jnp.where(row >= col, square, turned) + inflation
        square = jnp.where(row < col, square, turned)
        sys_ref[b:c, b:c] = jnp.where(row == col, diagonals[:, columns], square) + inflation
        sys_ref[b:c, a:b] = cross
        sys_ref[a:b, b:c] = cross.T
    cross = total(HALF, HALF)
    sys_ref[HALF:MEMBERS, 0:HALF] = cross
    sys_ref[0:HALF, HALF:MEMBERS] = cross.T
    rhs = jnp.concatenate([tail[0:1] + tail[4:5], tail[8:9] + tail[12:13]], axis=1)

    system = sys_ref[...]
    squares = jnp.sum(jnp.sum(system * system, axis=0, keepdims=True), axis=1, keepdims=True)
    norm = jnp.sqrt(squares)

    def dot(a, b):
        return jnp.dot(a[...], b[...], preferred_element_type=F32)

    def two_sweeps(w_ref, wb_ref):
        square = dot(tb_ref, tb_ref)
        sb_ref[...] = square.astype(BF16)
        ub_ref[...] = (0.0625 * square - 0.5625 * t_ref[...]).astype(BF16)
        w_ref[...] = 1.6875 * square - 2.4375 * t_ref[...]
        w = w_ref[...] + dot(ub_ref, sb_ref)
        w_ref[...] = w
        wb_ref[...] = w.astype(BF16)
        ub_ref[...] = (4.5 * w_ref[...] + dot(wb_ref, wb_ref)).astype(BF16)
        t = 5.0625 * t_ref[...] + dot(ub_ref, tb_ref)
        t_ref[...] = t
        tb_ref[...] = t.astype(BF16)

    t = system * (1.0 / norm)
    t_ref[...] = t
    tb_ref[...] = t.astype(BF16)
    two_sweeps(w_ref, wb_ref)
    two_sweeps(w2_ref, w2b_ref)
    w = 2.25 * (w_ref[...] + w2_ref[...]) + dot(wb_ref, w2b_ref)
    w_ref[...] = w
    wb_ref[...] = w.astype(BF16)
    w = 1.5 * w_ref[...] - 2.53125 * t_ref[...] - 0.5 * dot(wb_ref, tb_ref)

    row = lax.broadcasted_iota(jnp.int32, (MEMBERS, MEMBERS), 0)
    col = lax.broadcasted_iota(jnp.int32, (MEMBERS, MEMBERS), 1)
    root_inv = w + jnp.where(row == col, 1.5 * 5.0625, 0.0)
    half_step = jnp.sum(root_inv * rhs, axis=1, keepdims=True)
    mean_weight = jnp.sum(root_inv * half_step, axis=0, keepdims=True) / norm
    out_ref[...] = (jnp.sqrt((MEMBERS - 1.0) / norm) * root_inv + mean_weight).astype(BF16)


def update_kernel(transform_ref, state_ref, out_ref, dev_ref):
    column = my_column()

    def gather(i, acc):
        parts = [state_ref[i, column ^ w].astype(F32) for w in range(ROW_PATCHES)]
        block = jnp.concatenate(parts, axis=0)
        dev_ref[pl.ds(pl.multiple_of(i * 32, 32), 32)] = block.astype(BF16)
        return acc + jnp.sum(block.reshape(4, 8, CELLS), axis=0)

    acc = lax.fori_loop(0, 16, gather, jnp.zeros((8, CELLS), F32))
    centre = jnp.sum(acc, axis=0, keepdims=True) / MEMBERS
    dev_ref[...] = (dev_ref[...].astype(F32) - centre).astype(BF16)
    update = jnp.dot(transform_ref[...], dev_ref[...], preferred_element_type=F32)
    analysis = (centre + update).reshape(64, 8, CELLS)
    out_ref[:, 0] = analysis[:, 0:4].astype(BF16)
    out_ref[:, 1] = analysis[:, 4:8].astype(BF16)


def vmem(mebibytes):
    return pltpu.CompilerParams(vmem_limit_bytes=mebibytes * 2**20)


VMEM = pl.BlockSpec(memory_space=pltpu.VMEM)
HBM = pl.BlockSpec(memory_space=pltpu.HBM)
SMEM = pl.BlockSpec(memory_space=pltpu.SMEM)


def in_hbm(array):
    return pltpu.with_memory_space_constraint(array, pltpu.HBM)


def pallas(kernel, mebibytes, outs, in_specs, out_specs, scratch):
    return pl.pallas_call(
        kernel,
        out_shape=[jax.ShapeDtypeStruct(shape, dtype) for shape, dtype in outs],
        in_specs=in_specs,
        out_specs=out_specs,
        scratch_shapes=scratch,
        compiler_params=vmem(mebibytes),
    )


def shards(state_ens, obs_ens, obs_value, obs_class, loc_table, nbr_weight):
    obs = lax.all_to_all(
        obs_ens.reshape(4, 128, LOCAL_OBS), "mem", split_axis=1, concat_axis=0, tiled=False,
        axis_index_groups=[ORDER],
    ).reshape(64, 2, 4, LOCAL_OBS)
    values = jnp.stack([obs_value, lookup(obs_class, loc_table)])
    values = lax.ppermute(values, ("grp", "mem"), [(p, device_of(p)) for p in range(256)])

    part = (16, 4, CELLS)
    by_column = state_ens.reshape(4, 16, ROW_PATCHES, CELLS).transpose(1, 2, 0, 3)
    parts = list(pallas(
        split_kernel, 4, [(part, BF16)] * ROW_PATCHES, [HBM], [VMEM] * ROW_PATCHES,
        [pltpu.SemaphoreType.DMA((ROW_PATCHES,))],
    )(in_hbm(by_column)))
    for d in range(1, ROW_PATCHES):
        parts[d] = lax.ppermute(parts[d], "mem", [(k, k ^ d) for k in range(128)])
    (state,) = pallas(
        merge_kernel, 4, [((16, ROW_PATCHES, 4, CELLS), BF16)], [VMEM] * ROW_PATCHES, [HBM],
        [pltpu.SemaphoreType.DMA((ROW_PATCHES,))],
    )(*parts)
    state, obs, values = lax.optimization_barrier((state, obs, values))
    state = lax.all_to_all(
        state, "mem", split_axis=0, concat_axis=0, tiled=False,
        axis_index_groups=[ORDER[w::ROW_PATCHES] for w in range(ROW_PATCHES)],
    )

    packed = (PACKED, HALF)
    own, send = pallas(
        gram_kernel, 10, [(packed, F32), (packed, BF16)], [VMEM, VMEM], [VMEM, VMEM],
        [
            pltpu.VMEM((MEMBERS, LOCAL_OBS), BF16),
            pltpu.VMEM((MEMBERS + VEC, LOCAL_OBS), BF16),
        ],
    )(obs, values)
    received = []
    for (by, parity) in ((ROW_PATCHES, 0), (ROW_PATCHES, 1), (1, 1), (1, 0)):
        received.append(lax.ppermute(send, ("grp", "mem"), swaps(by, parity)))
    square = (MEMBERS, MEMBERS)
    (transform,) = pallas(
        solve_kernel, 16, [(square, BF16)], [SMEM] + [VMEM] * 5, [VMEM],
        [pltpu.VMEM(square, F32)] * 4 + [pltpu.VMEM(square, BF16)] * 5,
    )(nbr_weight, own, *received)
    (analysis,) = pallas(
        update_kernel, 8, [((64, 2, 4, CELLS), BF16)], [VMEM, VMEM], [VMEM],
        [pltpu.VMEM(square, BF16)],
    )(transform, state)
    back = lax.all_to_all(
        analysis.reshape(128, 4, CELLS), "mem", split_axis=0, concat_axis=1, tiled=False,
        axis_index_groups=[ORDER],
    )
    return back.reshape(4, 65536)


def solution(mesh):
    in_specs = (P("mem", "grp"), P("mem", "grp"), P(("grp", "mem")), P(("grp", "mem")), P(), P())
    out_specs = P("mem", "grp")
    return jax.shard_map(shards, mesh=mesh, in_specs=in_specs, out_specs=out_specs, check_vma=False)
```

```python
import jax
import jax.numpy as jnp
from jax import lax
from jax.experimental import pallas as pl
from jax.experimental.pallas import tpu as pltpu
from jax.sharding import PartitionSpec as P


MEMBERS = 512
CELLS = 512
LOCAL_OBS = 1024
ROW_PATCHES = 8
HALF = MEMBERS // 2
QUARTER = MEMBERS // 4
VEC = 16
PACKED = MEMBERS + VEC
F32 = jnp.float32
BF16 = jnp.bfloat16


def placement():
    order = []
    for row in range(16):
        z, step = row // 4, row % 4
        x = 3 - step if z % 2 == 0 else step
        order += [x * 32 + z * 8 + w for w in range(ROW_PATCHES)]
    return order


ORDER = placement()


def device_of(patch):
    return patch // 128 * 128 + ORDER[patch % 128]


def swaps(by, parity):
    pairs = []
    for p in range(256):
        row, column = p // ROW_PATCHES, p % ROW_PATCHES
        q = p + by
        if q < 256 and (by == ROW_PATCHES or q // ROW_PATCHES == row):
            if (row if by == ROW_PATCHES else column) % 2 == parity:
                pairs += [(device_of(p), device_of(q)), (device_of(q), device_of(p))]
    return pairs


def swap_weights(weight_ref):
    west, east, north, south = (weight_ref[k] for k in range(4))
    mem = lax.axis_index("mem")
    even_row = lax.rem(lax.div(mem, 32) + lax.div(mem, 8), 2) == 1
    even_column = lax.rem(mem, 2) == 0
    return (
        jnp.where(even_row, south, north),
        jnp.where(even_row, north, south),
        jnp.where(even_column, west, east),
        jnp.where(even_column, east, west),
    )


def lookup(classes, weight_table):
    codes = lax.broadcasted_iota(jnp.int32, (weight_table.shape[0], classes.shape[0]), 0)
    picked = jnp.where(codes == classes[None, :], weight_table.astype(F32)[:, None], 0.0)
    return jnp.sum(picked, axis=0)


def my_column():
    return lax.rem(lax.axis_index("mem"), ROW_PATCHES)


def split_kernel(state_ref, *rest):
    outs, sem = rest[:ROW_PATCHES], rest[ROW_PATCHES]
    copies = [
        pltpu.make_async_copy(state_ref.at[:, my_column() ^ d], outs[d], sem.at[d])
        for d in range(ROW_PATCHES)
    ]
    for copy in copies:
        copy.start()
    for copy in copies:
        copy.wait()


def merge_kernel(*refs):
    parts, out_ref, sem = refs[:ROW_PATCHES], refs[ROW_PATCHES], refs[ROW_PATCHES + 1]
    copies = [
        pltpu.make_async_copy(parts[d], out_ref.at[:, d], sem.at[d]) for d in range(ROW_PATCHES)
    ]
    for copy in copies:
        copy.start()
    for copy in copies:
        copy.wait()


def gather_rows(ref, rows_ref):
    width = rows_ref.shape[1]

    def step(i, acc):
        block = ref[pl.ds(i * 4, 4)].astype(F32)
        block = jnp.concatenate([block[:, 0], block[:, 1]], axis=1)
        rows_ref[pl.ds(pl.multiple_of(i * 32, 32), 32)] = block.reshape(32, width).astype(BF16)
        return acc + jnp.sum(block, axis=0)

    acc = lax.fori_loop(0, 16, step, jnp.zeros((8, width), F32), unroll=4)
    return jnp.sum(acc, axis=0, keepdims=True) / MEMBERS


def gram_kernel(obs_ref, val_ref, own_ref, send_ref, spread_ref, left_ref):
    centre = gather_rows(obs_ref, spread_ref)
    observed = val_ref[0:1]
    rates = val_ref[1:2]

    def step(i, carry):
        at = pl.ds(pl.multiple_of(i * 32, 32), 32)
        spread = (spread_ref[at].astype(F32) - centre).astype(BF16)
        spread_ref[at] = spread
        left_ref[at] = (spread.astype(F32) * rates).astype(BF16)
        return carry

    lax.fori_loop(0, 16, step, 0, unroll=4)
    innovation = (rates * (observed - centre)).astype(BF16)
    left_ref[pl.ds(MEMBERS, VEC)] = jnp.broadcast_to(innovation, (VEC, innovation.shape[1]))
    contract = (((1,), (1,)), ((), ()))
    first = lax.dot_general(
        left_ref[...], spread_ref[0:HALF], contract, preferred_element_type=F32
    )
    second = lax.dot_general(
        left_ref[HALF:], spread_ref[HALF:MEMBERS], contract, preferred_element_type=F32
    )
    row = lax.broadcasted_iota(jnp.int32, (QUARTER, QUARTER), 0)
    col = lax.broadcasted_iota(jnp.int32, (QUARTER, QUARTER), 1)

    def put(rows, columns, part):
        own_ref[rows, columns] = part
        send_ref[rows, columns] = part.astype(BF16)

    low, high = slice(0, QUARTER), slice(QUARTER, HALF)
    diagonals = []
    for part, columns in ((first, low), (second, high)):
        last = part[high, high]
        put(low, columns, jnp.where(row >= col, part[low, low], last.T))
        put(high, columns, part[high, low])
        diagonals.append(jnp.sum(jnp.where(row == col, last, 0.0), axis=0, keepdims=True))
    put(slice(HALF, MEMBERS), slice(0, HALF), first[HALF:MEMBERS])
    row = lax.broadcasted_iota(jnp.int32, (VEC, HALF), 0)
    tail = jnp.where(row < 8, first[MEMBERS:], second[HALF:])
    tail = jnp.where(row % 4 == 2, jnp.concatenate(diagonals, axis=1), tail)
    rounded = tail.astype(BF16).astype(F32)
    is_high = row % 8 < 4
    own_ref[MEMBERS:] = jnp.where(is_high, tail, 0.0)
    send_ref[MEMBERS:] = jnp.where(is_high, rounded, tail - rounded).astype(BF16)


def solve_kernel(
    weight_ref, own_ref, ns0_ref, ns1_ref, ew1_ref, ew0_ref, out_ref,
    sys_ref, t_ref, w_ref, w2_ref, tb_ref, wb_ref, w2b_ref, sb_ref, ub_ref,
):
    weights = swap_weights(weight_ref)

    def total(start, rows):
        at = pl.ds(start, rows)
        acc = own_ref[at]
        for k, ref in enumerate((ns0_ref, ns1_ref, ew1_ref, ew0_ref)):
            acc = acc + weights[k] * ref[at].astype(F32)
        return acc

    row = lax.broadcasted_iota(jnp.int32, (QUARTER, QUARTER), 0)
    col = lax.broadcasted_iota(jnp.int32, (QUARTER, QUARTER), 1)

    top, low, tail = total(0, QUARTER), total(QUARTER, QUARTER), total(MEMBERS, VEC)
    inflation = jnp.where(row == col, MEMBERS - 1.0, 0.0)
    diagonals = tail[2:3] + tail[6:7]
    for start, columns in ((0, slice(0, QUARTER)), (HALF, slice(QUARTER, HALF))):
        a, b, c = start, start + QUARTER, start + HALF
        square, cross = top[:, columns], low[:, columns]
        turned = square.T
        sys_ref[a:b, a:b] = jnp.where(row >= col, square, turned) + inflation
        square = jnp.where(row < col, square, turned)
        sys_ref[b:c, b:c] = jnp.where(row == col, diagonals[:, columns], square) + inflation
        sys_ref[b:c, a:b] = cross
        sys_ref[a:b, b:c] = cross.T
    cross = total(HALF, HALF)
    sys_ref[HALF:MEMBERS, 0:HALF] = cross
    sys_ref[0:HALF, HALF:MEMBERS] = cross.T
    rhs = jnp.concatenate([tail[0:1] + tail[4:5], tail[8:9] + tail[12:13]], axis=1)

    system = sys_ref[...]
    squares = jnp.sum(jnp.sum(system * system, axis=0, keepdims=True), axis=1, keepdims=True)
    norm = jnp.sqrt(squares)

    def dot(a, b):
        return jnp.dot(a[...], b[...], preferred_element_type=F32)

    def two_sweeps(w_ref, wb_ref):
        square = dot(tb_ref, tb_ref)
        sb_ref[...] = square.astype(BF16)
        ub_ref[...] = (0.0625 * square - 0.5625 * t_ref[...]).astype(BF16)
        w_ref[...] = 1.6875 * square - 2.4375 * t_ref[...]
        w = w_ref[...] + dot(ub_ref, sb_ref)
        w_ref[...] = w
        wb_ref[...] = w.astype(BF16)
        ub_ref[...] = (4.5 * w_ref[...] + dot(wb_ref, wb_ref)).astype(BF16)
        t = 5.0625 * t_ref[...] + dot(ub_ref, tb_ref)
        t_ref[...] = t
        tb_ref[...] = t.astype(BF16)

    t = system * (1.0 / norm)
    t_ref[...] = t
    tb_ref[...] = t.astype(BF16)
    two_sweeps(w_ref, wb_ref)
    two_sweeps(w2_ref, w2b_ref)
    w = 2.25 * (w_ref[...] + w2_ref[...]) + dot(wb_ref, w2b_ref)
    w_ref[...] = w
    wb_ref[...] = w.astype(BF16)
    w = 1.5 * w_ref[...] - 2.53125 * t_ref[...] - 0.5 * dot(wb_ref, tb_ref)

    row = lax.broadcasted_iota(jnp.int32, (MEMBERS, MEMBERS), 0)
    col = lax.broadcasted_iota(jnp.int32, (MEMBERS, MEMBERS), 1)
    root_inv = w + jnp.where(row == col, 1.5 * 5.0625, 0.0)
    half_step = jnp.sum(root_inv * rhs, axis=1, keepdims=True)
    mean_weight = jnp.sum(root_inv * half_step, axis=0, keepdims=True) / norm
    out_ref[...] = (jnp.sqrt((MEMBERS - 1.0) / norm) * root_inv + mean_weight).astype(BF16)


def update_kernel(transform_ref, state_ref, out_ref, dev_ref):
    column = my_column()

    def gather(i, acc):
        parts = [state_ref[i, column ^ w].astype(F32) for w in range(ROW_PATCHES)]
        block = jnp.concatenate(parts, axis=0)
        dev_ref[pl.ds(pl.multiple_of(i * 32, 32), 32)] = block.astype(BF16)
        return acc + jnp.sum(block.reshape(4, 8, CELLS), axis=0)

    acc = lax.fori_loop(0, 16, gather, jnp.zeros((8, CELLS), F32), unroll=4)
    centre = jnp.sum(acc, axis=0, keepdims=True) / MEMBERS
    dev_ref[...] = (dev_ref[...].astype(F32) - centre).astype(BF16)
    update = jnp.dot(transform_ref[...], dev_ref[...], preferred_element_type=F32)
    analysis = (centre + update).reshape(64, 8, CELLS)
    out_ref[:, 0] = analysis[:, 0:4].astype(BF16)
    out_ref[:, 1] = analysis[:, 4:8].astype(BF16)


def vmem(mebibytes):
    return pltpu.CompilerParams(vmem_limit_bytes=mebibytes * 2**20)


VMEM = pl.BlockSpec(memory_space=pltpu.VMEM)
HBM = pl.BlockSpec(memory_space=pltpu.HBM)
SMEM = pl.BlockSpec(memory_space=pltpu.SMEM)


def in_hbm(array):
    return pltpu.with_memory_space_constraint(array, pltpu.HBM)


def pallas(kernel, mebibytes, outs, in_specs, out_specs, scratch):
    return pl.pallas_call(
        kernel,
        out_shape=[jax.ShapeDtypeStruct(shape, dtype) for shape, dtype in outs],
        in_specs=in_specs,
        out_specs=out_specs,
        scratch_shapes=scratch,
        compiler_params=vmem(mebibytes),
    )


def shards(state_ens, obs_ens, obs_value, obs_class, loc_table, nbr_weight):
    obs = lax.all_to_all(
        obs_ens.reshape(4, 128, LOCAL_OBS), "mem", split_axis=1, concat_axis=0, tiled=False,
        axis_index_groups=[ORDER],
    ).reshape(64, 2, 4, LOCAL_OBS)
    values = jnp.stack([obs_value, lookup(obs_class, loc_table)])
    values = lax.ppermute(values, ("grp", "mem"), [(p, device_of(p)) for p in range(256)])

    part = (16, 4, CELLS)
    by_column = state_ens.reshape(4, 16, ROW_PATCHES, CELLS).transpose(1, 2, 0, 3)
    parts = list(pallas(
        split_kernel, 4, [(part, BF16)] * ROW_PATCHES, [HBM], [VMEM] * ROW_PATCHES,
        [pltpu.SemaphoreType.DMA((ROW_PATCHES,))],
    )(in_hbm(by_column)))
    for d in range(1, ROW_PATCHES):
        parts[d] = lax.ppermute(parts[d], "mem", [(k, k ^ d) for k in range(128)])
    (state,) = pallas(
        merge_kernel, 4, [((16, ROW_PATCHES, 4, CELLS), BF16)], [VMEM] * ROW_PATCHES, [HBM],
        [pltpu.SemaphoreType.DMA((ROW_PATCHES,))],
    )(*parts)
    state, obs, values = lax.optimization_barrier((state, obs, values))
    state = lax.all_to_all(
        state, "mem", split_axis=0, concat_axis=0, tiled=False,
        axis_index_groups=[ORDER[w::ROW_PATCHES] for w in range(ROW_PATCHES)],
    )

    packed = (PACKED, HALF)
    own, send = pallas(
        gram_kernel, 10, [(packed, F32), (packed, BF16)], [VMEM, VMEM], [VMEM, VMEM],
        [
            pltpu.VMEM((MEMBERS, LOCAL_OBS), BF16),
            pltpu.VMEM((MEMBERS + VEC, LOCAL_OBS), BF16),
        ],
    )(obs, values)
    received = []
    for (by, parity) in ((ROW_PATCHES, 0), (ROW_PATCHES, 1), (1, 1), (1, 0)):
        received.append(lax.ppermute(send, ("grp", "mem"), swaps(by, parity)))
    square = (MEMBERS, MEMBERS)
    (transform,) = pallas(
        solve_kernel, 16, [(square, BF16)], [SMEM] + [VMEM] * 5, [VMEM],
        [pltpu.VMEM(square, F32)] * 4 + [pltpu.VMEM(square, BF16)] * 5,
    )(nbr_weight, own, *received)
    (analysis,) = pallas(
        update_kernel, 8, [((64, 2, 4, CELLS), BF16)], [VMEM, VMEM], [VMEM],
        [pltpu.VMEM(square, BF16)],
    )(transform, state)
    back = lax.all_to_all(
        analysis.reshape(128, 4, CELLS), "mem", split_axis=0, concat_axis=1, tiled=False,
        axis_index_groups=[ORDER],
    )
    return back.reshape(4, 65536)


def solution(mesh):
    in_specs = (P("mem", "grp"), P("mem", "grp"), P(("grp", "mem")), P(("grp", "mem")), P(), P())
    out_specs = P("mem", "grp")
    return jax.shard_map(shards, mesh=mesh, in_specs=in_specs, out_specs=out_specs, check_vma=False)
```
